128 devices in a mesh: ctx: 32 (over y, x, core), head: 4 (over z).
Axes of the slice: x: 4, y: 4, z: 4, core: 2. Of those that a mesh axis runs over, the one named last changes fastest.
Arguments:
- query_raw: bfloat16 [16384, 2048], P('ctx', 'head'), may hold values from -120 to 120
- key_raw: bfloat16 [16384, 2048], P('ctx', 'head'), may hold values from -120 to 120
- value_raw: bfloat16 [16384, 4096], P('ctx', 'head'), may hold values from -120 to 120
- conv_query: bfloat16 [4, 2048], P(None, 'head'), may hold values from -3 to 3
- conv_key: bfloat16 [4, 2048], P(None, 'head'), may hold values from -3 to 3
- conv_value: bfloat16 [4, 4096], P(None, 'head'), may hold values from -3 to 3
- decay_log: float32 [32, 16384], P('head', 'ctx'), may hold values from -0.6 to 0, as said below
- write_beta: float32 [32, 16384], P('head', 'ctx'), may hold values from 0 to 1
- gate_input: bfloat16 [16384, 4096], P('ctx', 'head'), may hold values from -6 to 6
- norm_gain: float32 [128], replicated, may hold values from 0.5 to 1.5
- out_weight: bfloat16 [4096, 2048], P('head'), may hold values from -0.125 to 0.125
Outputs:
- mixed: bfloat16 [16384, 2048], P('ctx', 'head')
The draws below stay inside these ranges and needn't reach their ends.
Inputs may be any that keep to these rules, and one draw needn't show every extreme that they name: `decay_log`: natural logarithm of a decay factor.
All inputs are finite; a program needn't handle non-finite values.
Results may differ from the reference program's by a relative error of at most 0.014.
Values may be sent and summed in bfloat16 or wider, within the bound.
No kernel may reach another device: no remote copies, remote signals or barrier semaphores. Data moves between devices by JAX's collectives and lax.ppermute only.
A program may use at most 128 MiB of HBM per device.

```python
import math
import jax
import jax.numpy as jnp
from jax import lax

D_MODEL = 2048
HK = 16
VALUE_HEAD_COUNT = 32
DK = 128
DV = 128
CONV = 4
BLOCK = 64
TOK_DEV = 512
WINDOW_TOKENS = 16384
N_HEAD = 4


def gate_plan(key):
    parallel_lanes = jax.random.split(jax.random.fold_in(key, 31), 8)
    slow_share = 0.5
    gradual_heads = jax.random.uniform(parallel_lanes[0], (VALUE_HEAD_COUNT, 1)) < slow_share
    roughness = jax.random.uniform(parallel_lanes[1], (VALUE_HEAD_COUNT, WINDOW_TOKENS), minval=0.5, maxval=1.5)
    block_scale = jnp.exp(jax.random.uniform(parallel_lanes[2], (VALUE_HEAD_COUNT, WINDOW_TOKENS // TOK_DEV, 1), minval=math.log(0.5), maxval=math.log(2.0)))
    block_scale = jnp.broadcast_to(block_scale, (VALUE_HEAD_COUNT, WINDOW_TOKENS // TOK_DEV, TOK_DEV)).reshape(VALUE_HEAD_COUNT, WINDOW_TOKENS)
    fast_rate = jax.random.uniform(parallel_lanes[3], (VALUE_HEAD_COUNT, 1), minval=1.0 / 50.0, maxval=1.0 / 30.0)
    forget_speed = jnp.where(gradual_heads, 0.15 / WINDOW_TOKENS, fast_rate) * roughness * block_scale
    spike_positions = jax.random.randint(parallel_lanes[4], (3,), 0, WINDOW_TOKENS)
    spike_mask = jnp.any(jnp.arange(WINDOW_TOKENS)[None, :] == spike_positions[:, None], axis=0)[None, :] & gradual_heads
    spike_decrease = jnp.log(jax.random.uniform(parallel_lanes[5], (VALUE_HEAD_COUNT, WINDOW_TOKENS), minval=0.6, maxval=0.8))
    forget_factors = jnp.where(spike_mask, spike_decrease, -forget_speed)
    small_beta = 0.25 * DK / WINDOW_TOKENS * jax.random.uniform(parallel_lanes[6], (VALUE_HEAD_COUNT, WINDOW_TOKENS), minval=0.5, maxval=1.5)
    large_beta = jax.random.uniform(parallel_lanes[7], (VALUE_HEAD_COUNT, WINDOW_TOKENS), minval=0.3, maxval=0.9)
    beta_values = jnp.where(gradual_heads, jnp.minimum(small_beta, 0.5), large_beta)
    return (forget_factors, beta_values)


def draw_rows(key, width):
    parallel_lanes = jax.random.split(key, 3)
    row_scale = jnp.exp(jax.random.uniform(parallel_lanes[0], (WINDOW_TOKENS, 1), minval=0.0, maxval=math.log(10.0)))
    column_scale = jnp.exp(jax.random.uniform(parallel_lanes[1], (1, width), minval=math.log(0.5), maxval=math.log(2.0)))
    base_draw = jax.random.normal(parallel_lanes[2], (WINDOW_TOKENS, width))
    base_draw = jnp.clip(base_draw, -6.0, 6.0)
    return jnp.clip(base_draw * row_scale * column_scale, -120.0, 120.0)


def draw_query_raw(key, part):
    return draw_rows(jax.random.fold_in(key, 1), HK * DK).astype(jnp.bfloat16)


def draw_key_raw(key, part):
    return draw_rows(jax.random.fold_in(key, 2), HK * DK).astype(jnp.bfloat16)


def draw_value_raw(key, part):
    return draw_rows(jax.random.fold_in(key, 3), VALUE_HEAD_COUNT * DV).astype(jnp.bfloat16)


def draw_decay_log(key, part):
    return gate_plan(key)[0].astype(jnp.float32)


def draw_write_beta(key, part):
    return gate_plan(key)[1].astype(jnp.float32)


def spiked(values, own_key, source, target, shards_of, factor):
    owner, partner = [(jnp.arange(values.shape[position]) // (values.shape[position] // shards_of)).reshape([-1 if axis == position else 1 for axis in range(values.ndim)]) for position in (source, target)]
    chosen = jax.random.permutation(own_key, shards_of)[partner]
    strong = (owner == chosen) | (owner == (partner + shards_of // 2) % shards_of)
    return jnp.where(strong, factor * values, values)


def shard_levels(own_key, extent, cuts, smallest, top_value):
    def one(axis_at, parts):
        steps = jax.random.uniform(jax.random.fold_in(jax.random.fold_in(own_key, 6), axis_at), (parts,), jnp.float32, smallest / len(cuts), top_value / len(cuts))
        return jnp.repeat(jnp.exp(steps), extent[axis_at] // parts).reshape((-1,) + (1,) * (len(extent) - axis_at - 1))

    loudness = one(*cuts[0])
    for cut in cuts[1:]:
        loudness = loudness * one(*cut)
    return loudness


def centred(key, extent, deviation, reach, cuts=(), kind=jnp.bfloat16):
    values = deviation * jax.random.normal(key, extent, jnp.float32)
    if cuts:
        values = values * shard_levels(key, extent, cuts, -0.22, 0.18)
    return jnp.clip(values, -reach, reach).astype(kind)


def noise_with(rng, dims, scale, most, pieces, heavy, kind=jnp.bfloat16):
    values = scale * jax.random.normal(rng, dims, jnp.float32)
    if pieces:
        values = values * shard_levels(rng, dims, pieces, -0.22, 0.18)
    return jnp.clip(spiked(values, jax.random.fold_in(rng, 3), *heavy), -most, most).astype(kind)


def setup_inputs(seed: int = 0) -> dict:
    seeds = jax.random.split(jax.random.key(seed), 12)
    return {
        "query_raw": draw_query_raw(jax.random.fold_in(seeds[11], 71), 0),
        "key_raw": draw_key_raw(jax.random.fold_in(seeds[11], 71), 0),
        "value_raw": draw_value_raw(jax.random.fold_in(seeds[11], 71), 0),
        "conv_query": centred(seeds[3], (CONV, HK * DK), 0.5, 3.0, ((1, 4),)),
        "conv_key": centred(seeds[4], (CONV, HK * DK), 0.5, 3.0, ((1, 4),)),
        "conv_value": centred(seeds[5], (CONV, VALUE_HEAD_COUNT * DV), 0.5, 3.0, ((1, 4),)),
        "decay_log": draw_decay_log(jax.random.fold_in(seeds[11], 71), 0),
        "write_beta": draw_write_beta(jax.random.fold_in(seeds[11], 71), 0),
        "gate_input": centred(seeds[8], (WINDOW_TOKENS, VALUE_HEAD_COUNT * DV), 1.0, 6.0, ((0, 32), (1, 4))),
        "norm_gain": jnp.clip(jax.random.uniform(seeds[9], (DV,), jnp.float32, 0.5, 1.5), 0.5, 1.5),
        "out_weight": noise_with(seeds[10], (VALUE_HEAD_COUNT * DV, D_MODEL), (VALUE_HEAD_COUNT * DV) ** -0.5, 0.125, ((0, 4),), (0, 1, 4, 2.0)),
    }


highest = lax.Precision.HIGHEST

def conv_silu(raw_rows, conv_weight):
    widths = conv_weight.shape[0]
    length = raw_rows.shape[0]
    padded = jnp.concatenate([jnp.zeros((widths - 1, raw_rows.shape[1]), jnp.float32), raw_rows.astype(jnp.float32)], 0)
    weights = conv_weight.astype(jnp.float32)
    running = jnp.zeros((length, raw_rows.shape[1]), jnp.float32)
    for offset in range(widths):
        running = running + weights[offset] * padded[offset:offset + length]
    return jax.nn.silu(running)

def unit_rows(values):
    return values * lax.rsqrt(lax.optimization_barrier(jnp.sum(values * values, -1, keepdims=True)) + 1e-06)

def prepare(key_block, value_block, cumulative, beta_blocks):
    length = key_block.shape[-2]
    inner_keys = jnp.einsum('...id,...jd->...ij', key_block, key_block, precision=highest)
    positions = jnp.arange(length)
    strict_lower = positions[:, None] > positions[None, :]
    causal = positions[:, None] >= positions[None, :]
    spread = jnp.exp(jnp.where(causal, cumulative[..., :, None] - cumulative[..., None, :], 0.0))
    lower_part = jnp.where(strict_lower, beta_blocks[..., :, None] * inner_keys * spread, 0.0)
    system = jnp.eye(length, dtype=jnp.float32) + lower_part
    key_mix = jax.scipy.linalg.solve_triangular(system, (beta_blocks * jnp.exp(cumulative))[..., None] * key_block, lower=True)
    value_mix = jax.scipy.linalg.solve_triangular(system, beta_blocks[..., None] * value_block, lower=True)
    return (key_mix, value_mix, spread, causal)

def block_outputs(carry_state, query_block, key_block, key_mix, value_mix, cumulative, spread, causal):
    fresh_values = value_mix - jnp.einsum('hcd,hvd->hcv', key_mix, carry_state, precision=highest)
    scores = jnp.where(causal, jnp.einsum('hid,hjd->hij', query_block, key_block, precision=highest) * spread, 0.0)
    result = jnp.einsum('hcd,hvd->hcv', query_block * jnp.exp(cumulative)[..., None], carry_state, precision=highest)
    result = result + jnp.einsum('hij,hjv->hiv', scores, fresh_values, precision=highest)
    last_cum = cumulative[:, -1]
    carried = jnp.exp(last_cum[:, None] - cumulative)[..., None] * fresh_values
    carry_state = jnp.exp(last_cum)[:, None, None] * carry_state + jnp.einsum('hcv,hcd->hvd', carried, key_block, precision=highest)
    return (carry_state, result)

def reference(query_raw, key_raw, value_raw, conv_query, conv_key, conv_value, decay_log, write_beta, gate_input, norm_gain, out_weight):
    head_ratio = VALUE_HEAD_COUNT // HK
    block_count = WINDOW_TOKENS // BLOCK
    queries = unit_rows(conv_silu(query_raw, conv_query).reshape(WINDOW_TOKENS, HK, DK)) * DK ** (-0.5)
    key_unit = unit_rows(conv_silu(key_raw, conv_key).reshape(WINDOW_TOKENS, HK, DK))
    values = conv_silu(value_raw, conv_value).reshape(WINDOW_TOKENS, VALUE_HEAD_COUNT, DV)

    def blocks(array, heads, width):
        return array.reshape(block_count, BLOCK, heads, width).transpose(0, 2, 1, 3)
    cumulative = jnp.cumsum(decay_log.reshape(VALUE_HEAD_COUNT, block_count, BLOCK).transpose(1, 0, 2), axis=-1)
    beta_blocks = write_beta.reshape(VALUE_HEAD_COUNT, block_count, BLOCK).transpose(1, 0, 2)

    def advance(carry_state, inputs):
        query_block, key_block, value_block, cumul_block, beta_block = inputs
        query_block = jnp.repeat(query_block, head_ratio, axis=0)
        key_block = jnp.repeat(key_block, head_ratio, axis=0)
        key_mix, value_mix, spread, causal = prepare(key_block, value_block, cumul_block, beta_block)
        return block_outputs(carry_state, query_block, key_block, key_mix, value_mix, cumul_block, spread, causal)
    initial = jnp.zeros((VALUE_HEAD_COUNT, DV, DK), jnp.float32)
    unused, outputs = lax.scan(advance, initial, (blocks(queries, HK, DK), blocks(key_unit, HK, DK), blocks(values, VALUE_HEAD_COUNT, DV), cumulative, beta_blocks))
    heads_out = outputs.transpose(0, 2, 1, 3).reshape(WINDOW_TOKENS, VALUE_HEAD_COUNT, DV)
    normed = heads_out * lax.rsqrt(lax.optimization_barrier(jnp.mean(heads_out * heads_out, -1, keepdims=True)) + 1e-06)
    gated = normed * norm_gain * jax.nn.silu(gate_input.astype(jnp.float32).reshape(WINDOW_TOKENS, VALUE_HEAD_COUNT, DV))
    hidden = gated.astype(jnp.bfloat16).reshape(WINDOW_TOKENS, VALUE_HEAD_COUNT * DV)
    group_width = VALUE_HEAD_COUNT * DV // N_HEAD
    running = jnp.zeros((WINDOW_TOKENS, D_MODEL), jnp.float32)
    for member in range(N_HEAD):
        partial_sum = jnp.dot(hidden[:, member * group_width:(member + 1) * group_width].astype(jnp.float32), out_weight[member * group_width:(member + 1) * group_width].astype(jnp.float32), preferred_element_type=jnp.float32)
        rounded = lax.optimization_barrier(partial_sum.astype(jnp.bfloat16))
        running = running + rounded.astype(jnp.float32)
    return running.astype(jnp.bfloat16)
```

```python
import jax
import jax.numpy as jnp
from jax import lax
from jax.experimental import pallas as pl
from jax.experimental.pallas import tpu as pltpu
from jax.sharding import PartitionSpec as P

DK = 128
DV = 128
CHUNK = 128
ROW = 8
EXTRA = 16
VMEM_BYTES = 56 * 1024 * 1024

f32 = jnp.float32
bf16 = jnp.bfloat16
highest = lax.Precision.HIGHEST


def mm(a, b, dims=((1,), (0,))):
    return lax.dot_general(a, b, (dims, ((), ())), preferred_element_type=f32)


def mm_exact(a, b, dims=((1,), (0,))):
    return lax.dot_general(a, b, (dims, ((), ())), preferred_element_type=f32, precision=highest)


NT = ((1,), (1,))
TN = ((0,), (0,))


def silu(x):
    return x / (1.0 + jnp.exp(-x))


def split3(x):
    hi = x.astype(bf16)
    rest = x - hi.astype(f32)
    mid = rest.astype(bf16)
    low = (rest - mid.astype(f32)).astype(bf16)
    return hi, mid, low


def prep_kernel(
    q_ref, k_ref, v_ref, rim_ref, cq_ref, ck_ref, cv_ref, dl_ref, wb_ref,
    o_ref, qe_ref, x_ref,
    pad, ks, qs, vs, lm, tm, rm, am, zt, gs,
):
    tokens, qw = q_ref.shape
    vw = v_ref.shape[1]
    key_heads = qw // DK
    heads = vw // DV
    ratio = heads // key_heads
    c = CHUNK
    ii = lax.broadcasted_iota(jnp.int32, (c, c), 0)
    jj = lax.broadcasted_iota(jnp.int32, (c, c), 1)
    xor = jnp.where(ii >= jj, ii ^ jj, -1)
    lower = (ii >= jj).astype(f32)
    upper = (ii <= jj).astype(f32)
    eye = (ii == jj).astype(f32)
    wq = cq_ref[...].astype(f32)
    wk = ck_ref[...].astype(f32)
    wv = cv_ref[...].astype(f32)
    pad[0:8, :] = rim_ref[...].astype(f32)
    zt[...] = jnp.zeros_like(zt)
    gs[...] = jnp.zeros_like(gs)

    def conv(col, w, wcol):
        acc = w[0:1, wcol : wcol + 128] * pad[5 : 5 + c, col : col + 128]
        for j in range(1, 4):
            acc = acc + w[j : j + 1, wcol : wcol + 128] * pad[5 + j : 5 + j + c, col : col + 128]
        return silu(acc)

    def unit(x):
        return x * lax.rsqrt(jnp.sum(x * x, -1, keepdims=True) + 1e-06)

    def chunk(b, unused):
        base = pl.multiple_of(b * c, c)
        rows = pl.ds(base, c)
        pad[8 : 8 + c, 0:qw] = q_ref[rows, :].astype(f32)
        pad[8 : 8 + c, qw : 2 * qw] = k_ref[rows, :].astype(f32)
        pad[8 : 8 + c, 2 * qw : 2 * qw + vw] = v_ref[rows, :].astype(f32)
        for h in range(key_heads):
            qs[h] = unit(conv(h * DK, wq, h * DK)) * DK ** (-0.5)
            ks[h] = unit(conv(qw + h * DK, wk, h * DK))
        for h in range(heads):
            vs[h] = conv(2 * qw + h * DV, wv, h * DV)
        pad[0:8, :] = pad[c : c + 8, :]

        dl = dl_ref[:, rows]
        wb = wb_ref[:, rows]
        c_row = mm_exact(dl, upper)
        c_col = mm_exact(lower, dl, NT)
        b_col = mm_exact(eye, wb, NT)
        last = c_col[c - 1 : c, :]
        ec = jnp.exp(c_col)
        be = b_col * ec
        tail = jnp.exp(last - c_col)
        g0 = gs[0:1, 0:heads]
        gam = jnp.broadcast_to(jnp.exp(g0), (c, heads))
        eg = jnp.exp(c_col + g0)
        el = jnp.broadcast_to(jnp.exp(last), (c, heads))
        gs[0:1, 0:heads] = g0 + last

        for kh in range(key_heads):
            kb = ks[kh].astype(bf16)
            qb = qs[kh].astype(bf16)
            gram = mm(kb, kb, NT)
            qk = mm(qb, kb, NT)
            for r in range(ratio):
                h = kh * ratio + r
                diff = c_col[:, h : h + 1] - c_row[h : h + 1, :]
                spread = jnp.exp(jnp.where(xor >= 0, diff, -1e30))
                low = b_col[:, h : h + 1] * gram * spread
                lm[h] = low
                am[h] = (qk * spread).astype(bf16)
                tm[h] = (eye - jnp.where(xor == 1, low, 0.0)).astype(bf16)
        s = 2
        while s < c:
            pick = (xor >= s) & (xor < 2 * s)
            for h in range(heads):
                rm[h] = mm(jnp.where(pick, lm[h], 0.0).astype(bf16), tm[h]).astype(bf16)
            for h in range(heads):
                tm[h] = tm[h] - mm(tm[h], rm[h]).astype(bf16)
            s *= 2
        for h in range(heads):
            kh = h // ratio
            k = ks[kh]
            q = qs[kh]
            rhs = jnp.concatenate([b_col[:, h : h + 1] * vs[h], be[:, h : h + 1] * k], 1).astype(bf16)
            uw = mm(tm[h], rhs)
            w = uw[:, DV:]
            z = zt[h]
            zb = z.astype(bf16)
            fresh = jnp.concatenate([uw[:, :DV], gam[:, h : h + 1] * w], 1) - mm(w.astype(bf16), zb)
            out = mm((ec[:, h : h + 1] * q).astype(bf16), zb) + mm(am[h], fresh.astype(bf16))
            o_ref[rows, h * DV : (h + 1) * DV] = out[:, :DV]
            qe_ref[rows, h * DK : (h + 1) * DK] = (eg[:, h : h + 1] * q - out[:, DV:]).astype(bf16)
            zt[h] = el[:, h : h + 1] * z + mm(
                k.astype(bf16), (tail[:, h : h + 1] * fresh).astype(bf16), TN
            )
        return unused

    lax.fori_loop(0, tokens // c, chunk, 0)
    total = jnp.broadcast_to(gs[0:1, 0:heads], (EXTRA, heads))
    row = lax.broadcasted_iota(jnp.int32, (EXTRA, DV), 0)
    for h in range(heads):
        z = zt[h]
        x_ref[h, 0:DK, :] = z[:, :DV].astype(bf16)
        x_ref[h, DK : 2 * DK, :] = z[:, DV:].astype(bf16)
        full = jnp.broadcast_to(total[:, h : h + 1], (EXTRA, DV))
        hi, mid, low = split3(full)
        x_ref[h, 2 * DK : 2 * DK + EXTRA, :] = jnp.where(
            row == 0, hi.astype(f32), jnp.where(row == 1, mid.astype(f32), jnp.where(row == 2, low.astype(f32), 0.0))
        ).astype(bf16)


def prep(q, k, v, rim, cq, ck, cv, dl, wb):
    tokens, qw = q.shape
    vw = v.shape[1]
    kh, h = qw // DK, vw // DV
    c = CHUNK
    return pl.pallas_call(
        prep_kernel,
        out_shape=(
            jax.ShapeDtypeStruct((tokens, vw), f32),
            jax.ShapeDtypeStruct((tokens, h * DK), bf16),
            jax.ShapeDtypeStruct((h, 2 * DK + EXTRA, DV), bf16),
        ),
        scratch_shapes=[
            pltpu.VMEM((c + 8, 2 * qw + vw), f32),
            pltpu.VMEM((kh, c, DK), f32),
            pltpu.VMEM((kh, c, DK), f32),
            pltpu.VMEM((h, c, DV), f32),
            pltpu.VMEM((h, c, c), f32),
            pltpu.VMEM((h, c, c), bf16),
            pltpu.VMEM((h, c, c), bf16),
            pltpu.VMEM((h, c, c), bf16),
            pltpu.VMEM((h, DK, DV + DK), f32),
            pltpu.VMEM((8, 128), f32),
        ],
        compiler_params=pltpu.CompilerParams(vmem_limit_bytes=VMEM_BYTES),
        name="prep",
    )(q, k, v, rim, cq, ck, cv, dl, wb)


def log_decay(ref, at):
    rows = ref[at, 2 * DK : 2 * DK + EXTRA, :].astype(f32)
    return rows[0:1, :] + rows[1:2, :] + rows[2:3, :]


def row_kernel(x_ref, pre_ref, g_ref, out_ref):
    count = x_ref.shape[0]
    z = jnp.zeros((DK, DV + DK), f32)
    g = jnp.zeros((1, DV), f32)
    for i in range(count):
        pre_ref[i] = z
        g_ref[i] = jnp.broadcast_to(g, (8, DV))
        step = log_decay(x_ref, i)
        d = x_ref[i, DK : 2 * DK, :]
        scale = jnp.broadcast_to(jnp.exp(step), (DK, DV))
        past = jnp.broadcast_to(jnp.exp(g), (DK, DV))
        add = jnp.concatenate([x_ref[i, 0:DK, :].astype(f32), past * d.astype(f32)], 1)
        z = jnp.concatenate([scale, scale], 1) * z - mm(d, z.astype(bf16)) + add
        g = g + step
    out_ref[0:DK, :] = z[:, :DV].astype(bf16)
    out_ref[DK : 2 * DK, :] = z[:, DV:].astype(bf16)
    row = lax.broadcasted_iota(jnp.int32, (EXTRA, DV), 0)
    hi, mid, low = split3(jnp.broadcast_to(g, (EXTRA, DV)))
    out_ref[2 * DK : 2 * DK + EXTRA, :] = jnp.where(
        row == 0, hi.astype(f32), jnp.where(row == 1, mid.astype(f32), jnp.where(row == 2, low.astype(f32), 0.0))
    ).astype(bf16)


def row_prefix(x):
    count = x.shape[0]
    return pl.pallas_call(
        row_kernel,
        out_shape=(
            jax.ShapeDtypeStruct((count, DK, DV + DK), f32),
            jax.ShapeDtypeStruct((count, 8, DV), f32),
            jax.ShapeDtypeStruct((2 * DK + EXTRA, DV), bf16),
        ),
        name="row_prefix",
    )(x)


def start_kernel(y_ref, a_ref, b_ref, c_ref, pre_ref, g_ref, out_ref):
    count = pre_ref.shape[0]
    s = jnp.zeros((DK, DV), f32)
    y = y_ref[0]
    for back, ref in ((3, a_ref), (2, b_ref), (1, c_ref)):
        rows = ref[2 * DK : 2 * DK + EXTRA, :].astype(f32)
        step = rows[0:1, :] + rows[1:2, :] + rows[2:3, :]
        scale = jnp.broadcast_to(jnp.exp(step), (DK, DV))
        after = scale * s - mm(ref[DK : 2 * DK, :], s.astype(bf16)) + ref[0:DK, :].astype(f32)
        s = jnp.where(y >= back, after, s)
    sb = s.astype(bf16)
    for i in range(count):
        z = pre_ref[i]
        scale = jnp.broadcast_to(jnp.exp(g_ref[i, 0:1, :]), (DK, DV))
        out_ref[i] = (scale * s - mm(z[:, DV:].astype(bf16), sb) + z[:, :DV]).astype(bf16)


def start_states(y, a, b, c, pre, g):
    count = pre.shape[0]
    return pl.pallas_call(
        start_kernel,
        in_specs=[pl.BlockSpec(memory_space=pltpu.SMEM)] + [pl.BlockSpec(memory_space=pltpu.VMEM)] * 5,
        out_shape=jax.ShapeDtypeStruct((count, DK, DV), bf16),
        name="start_states",
    )(y, a, b, c, pre, g)


def hidden_kernel(col_ref, o_ref, qe_ref, s_ref, gate_ref, gain_ref, w_ref, hid_ref, p_ref):
    heads = s_ref.shape[0]
    tokens = o_ref.shape[0]
    gain = gain_ref[...]
    for h in range(heads):
        cols = slice(h * DV, (h + 1) * DV)
        x = o_ref[:, cols] + mm(qe_ref[:, cols], s_ref[h])
        x = x * lax.rsqrt(jnp.mean(x * x, -1, keepdims=True) + 1e-06)
        hid_ref[:, cols] = (x * gain * silu(gate_ref[:, cols].astype(f32))).astype(bf16)
    p_ref[...] = mm(hid_ref[...], w_ref[...]).astype(bf16)


def hidden_part(col, o, qe, s, gate, gain, w):
    tokens, vw = o.shape
    width = w.shape[1] // 4
    full = lambda shape: pl.BlockSpec(shape, lambda i, c: (0,) * len(shape))
    return pl.pallas_call(
        hidden_kernel,
        grid_spec=pltpu.PrefetchScalarGridSpec(
            num_scalar_prefetch=1,
            grid=(1,),
            in_specs=[
                full(o.shape), full(qe.shape), full(s.shape), full(gate.shape), full(gain.shape),
                pl.BlockSpec((vw, width), lambda i, c: (0, c[0])),
            ],
            out_specs=[full((tokens, vw)), full((tokens, width))],
        ),
        out_shape=(
            jax.ShapeDtypeStruct((tokens, vw), bf16),
            jax.ShapeDtypeStruct((tokens, width), bf16),
        ),
        compiler_params=pltpu.CompilerParams(vmem_limit_bytes=VMEM_BYTES),
        name="hidden_part",
    )(col, o, qe, s, gate, gain, w)


def part_kernel(col_ref, hid_ref, w_ref, p_ref):
    p_ref[...] = mm(hid_ref[...], w_ref[...]).astype(bf16)


def part(col, hid, w):
    tokens, vw = hid.shape
    width = w.shape[1] // 4
    return pl.pallas_call(
        part_kernel,
        grid_spec=pltpu.PrefetchScalarGridSpec(
            num_scalar_prefetch=1,
            grid=(1,),
            in_specs=[
                pl.BlockSpec((tokens, vw), lambda i, c: (0, 0)),
                pl.BlockSpec((vw, width), lambda i, c: (0, c[0])),
            ],
            out_specs=pl.BlockSpec((tokens, width), lambda i, c: (0, 0)),
        ),
        out_shape=jax.ShapeDtypeStruct((tokens, width), bf16),
        compiler_params=pltpu.CompilerParams(vmem_limit_bytes=VMEM_BYTES),
        name="part",
    )(col, hid, w)


def body(q, k, v, cq, ck, cv, decay_log, write_beta, gate, gain, out_weight):
    tokens = q.shape[0]
    ctx = lax.axis_size("ctx")
    rows = ctx // ROW
    idx = lax.axis_index("ctx")
    z = lax.axis_index("head")
    tails = jnp.concatenate([q[tokens - 8 :], k[tokens - 8 :], v[tokens - 8 :]], 1)
    rim = lax.ppermute(tails, "ctx", [(i, i + 1) for i in range(ctx - 1)])
    o, qe, x = prep(q, k, v, rim, cq, ck, cv, decay_log, write_beta)
    groups = [[y * ROW + j for j in range(ROW)] for y in range(rows)]
    mine = lax.all_to_all(x, "ctx", 0, 0, axis_index_groups=groups, tiled=True)
    pre, g, whole = row_prefix(mine)

    def from_back(d):
        return lax.ppermute(whole, "ctx", [(i, (i + d * ROW) % ctx) for i in range(ctx)])

    s_mine = start_states((idx // ROW).reshape(1), from_back(3), from_back(2), from_back(1), pre, g)
    s = lax.all_to_all(s_mine, "ctx", 0, 0, axis_index_groups=groups, tiled=True)
    col = lambda d: ((z + d) % 4).reshape(1)
    ring = lambda d: [(i, (i + d) % 4) for i in range(4)]
    hid, p2 = hidden_part(col(2), o, qe, s, gate, gain.reshape(1, DV), out_weight)
    r2 = lax.ppermute(p2, "head", ring(2))
    r1 = lax.ppermute(part(col(1), hid, out_weight), "head", ring(1))
    r3 = lax.ppermute(part(col(3), hid, out_weight), "head", ring(3))
    p0 = part(col(0), hid, out_weight)
    total = p0.astype(f32) + r1.astype(f32) + r2.astype(f32) + r3.astype(f32)
    return total.astype(bf16)


def solution(mesh):
    return jax.shard_map(
        body,
        mesh=mesh,
        in_specs=(
            P("ctx", "head"), P("ctx", "head"), P("ctx", "head"),
            P(None, "head"), P(None, "head"), P(None, "head"),
            P("head", "ctx"), P("head", "ctx"), P("ctx", "head"), P(), P("head", None),
        ),
        out_specs=P("ctx", "head"),
        check_vma=False,
    )
```

```python
import functools

import jax
import jax.numpy as jnp
from jax import lax
from jax.experimental import pallas as pl
from jax.experimental.pallas import tpu as pltpu
from jax.sharding import PartitionSpec as P

DK = 128
DV = 128
CHUNK = 128
ROW = 8
EXTRA = 16
SUB = 16
GROUP = 16

f32 = jnp.float32
bf16 = jnp.bfloat16
highest = lax.Precision.HIGHEST


def mm(a, b, dims=((1,), (0,))):
    return lax.dot_general(a, b, (dims, ((), ())), preferred_element_type=f32)


def mm_exact(a, b, dims=((1,), (0,))):
    return lax.dot_general(a, b, (dims, ((), ())), preferred_element_type=f32, precision=highest)


NT = ((1,), (1,))
TN = ((0,), (0,))


SMEM_SPEC = pl.BlockSpec(memory_space=pltpu.SMEM)
VMEM_SPEC = pl.BlockSpec(memory_space=pltpu.VMEM)


def params(mib):
    return pltpu.CompilerParams(vmem_limit_bytes=mib * 1024 * 1024)


def local(x):
    return pltpu.with_memory_space_constraint(x, pltpu.MemorySpace.VMEM)


def far(x):
    return pltpu.with_memory_space_constraint(x, pltpu.MemorySpace.HBM)


def silu(x):
    return x / (1.0 + jnp.exp(-x))


def split3(x):
    hi = x.astype(bf16)
    rest = x - hi.astype(f32)
    mid = rest.astype(bf16)
    low = (rest - mid.astype(f32)).astype(bf16)
    return hi, mid, low


def extras(row):
    full = jnp.broadcast_to(row, (EXTRA, row.shape[1]))
    at = lax.broadcasted_iota(jnp.int32, full.shape, 0)
    hi, mid, low = (part.astype(f32) for part in split3(full))
    return jnp.where(at == 0, hi, jnp.where(at == 1, mid, jnp.where(at == 2, low, 0.0))).astype(bf16)


def tails_kernel(q_ref, k_ref, v_ref, out_ref):
    qw = q_ref.shape[1]
    out_ref[:, 0:qw] = q_ref[...]
    out_ref[:, qw : 2 * qw] = k_ref[...]
    out_ref[:, 2 * qw :] = v_ref[...]


def tails(q, k, v):
    last = q.shape[0] // 8 - 1
    spec = lambda a: pl.BlockSpec((8, a.shape[1]), lambda i: (last, 0))
    width = q.shape[1] + k.shape[1] + v.shape[1]
    return pl.pallas_call(
        tails_kernel,
        grid=(1,),
        in_specs=[spec(q), spec(k), spec(v)],
        out_specs=VMEM_SPEC,
        out_shape=pltpu.VMEM((8, width), bf16),
        name="tails",
    )(q, k, v)


def tile_of(t, q_ref, k_ref, v_ref):
    col, qw = t * 128, q_ref.shape[1]
    if col < qw:
        return q_ref, col
    if col < 2 * qw:
        return k_ref, col - qw
    return v_ref, col - 2 * qw


def load_taps(taps, cq_ref, ck_ref, cv_ref):
    for t in range(taps.shape[0] // 4):
        src, at = tile_of(t, cq_ref, ck_ref, cv_ref)
        w = src[:, at : at + 128].astype(f32)
        for j in range(4):
            taps[t * 4 + j] = jnp.broadcast_to(w[j : j + 1, :], (8, 128))


def conv_tile(pad, taps, tile, key_heads, put):
    stride = CHUNK // 8
    w = [taps[tile * 4 + j] for j in range(4)]
    x = [pad[tile, pl.ds(8 + v, 8, stride=stride), :] for v in range(-3, stride)]
    for v in range(stride):
        y = silu(w[0] * x[v] + w[1] * x[v + 1] + w[2] * x[v + 2] + w[3] * x[v + 3])
        if tile < 2 * key_heads:
            scale = DK ** (-0.5) if tile < key_heads else 1.0
            y = y * (lax.rsqrt(jnp.sum(y * y, -1, keepdims=True) + 1e-06) * scale)
        put(pl.ds(v, 8, stride=stride), y)


def acts_kernel(*refs):
    hbm, (out_ref, taps, pad, done), local_refs, sem = refs[:6], refs[6:10], refs[10:16], refs[16]
    fetches = [pltpu.make_async_copy(a, b, sem.at[n]) for n, (a, b) in enumerate(zip(hbm, local_refs))]
    for fetch in fetches:
        fetch.start()
    for fetch in fetches:
        fetch.wait()
    q_ref, k_ref, v_ref, cq_ref, ck_ref, cv_ref = local_refs
    tokens, qw = q_ref.shape
    c = CHUNK
    tiles = pad.shape[0]
    key_heads = qw // DK
    load_taps(taps, cq_ref, ck_ref, cv_ref)
    for t in range(tiles):
        src, at = tile_of(t, q_ref, k_ref, v_ref)
        raw = src[0:c, at : at + 128]
        out_ref[t, 0:c, :] = raw
        pad[t, 0:8, :] = raw[c - 8 :, :].astype(f32)

    def chunk(b, unused):
        rows = pl.ds(pl.multiple_of(b * c, c), c)
        for t in range(tiles):
            src, at = tile_of(t, q_ref, k_ref, v_ref)
            pad[t, 8 : 8 + c, :] = src[rows, at : at + 128].astype(f32)
        for t in range(tiles):

            def put(where, y):
                done[t, where, :] = y

            conv_tile(pad, taps, t, key_heads, put)
        for t in range(tiles):
            out_ref[t, rows, :] = done[t].astype(bf16)
            pad[t, 0:8, :] = pad[t, c : c + 8, :]
        return unused

    lax.fori_loop(1, tokens // c, chunk, 0)


def acts(q, k, v, cq, ck, cv):
    tokens = q.shape[0]
    tiles = (2 * q.shape[1] + v.shape[1]) // 128
    return pl.pallas_call(
        acts_kernel,
        in_specs=[pl.BlockSpec(memory_space=pl.ANY)] * 6,
        out_shape=[pltpu.VMEM((tiles, tokens, 128), bf16), pltpu.VMEM((tiles * 4, 8, 128), f32)],
        scratch_shapes=[
            pltpu.VMEM((tiles, CHUNK + 8, 128), f32),
            pltpu.VMEM((tiles, CHUNK, 128), f32),
        ]
        + [pltpu.VMEM(x.shape, x.dtype) for x in (q, k, v, cq, ck, cv)]
        + [pltpu.SemaphoreType.DMA((6,))],
        compiler_params=params(12),
        name="acts",
    )(*(far(x) for x in (q, k, v, cq, ck, cv)))


def prep_kernel(
    act_ref, taps, rim_ref, dl_ref, wb_ref,
    o_ref, qe_ref, x_ref,
    pad, fresh0, act0, cols, crow, lm, tm, qa, ke, kt, bv, gams, els, yb, fb, zt, gs,
):
    tiles, tokens, _ = act_ref.shape
    heads = dl_ref.shape[0]
    key_heads = (tiles - heads) // 2
    ratio = heads // key_heads
    c = CHUNK
    ii = lax.broadcasted_iota(jnp.int32, (c, c), 0)
    jj = lax.broadcasted_iota(jnp.int32, (c, c), 1)
    xor = jnp.where(ii >= jj, ii ^ jj, -1)
    lower = (ii >= jj).astype(f32)
    upper = (ii <= jj).astype(f32)
    eye = (ii == jj).astype(f32)
    ones = jnp.ones((c, c), f32)
    ri = lax.broadcasted_iota(jnp.int32, (SUB, c), 0)
    ci = lax.broadcasted_iota(jnp.int32, (SUB, c), 1)
    cx = jnp.where(ri >= ci % SUB, ri ^ (ci % SUB), -1)
    band16 = [(ci // SUB == b).astype(f32).astype(bf16) for b in range(c // SUB)]
    zt[...] = jnp.zeros_like(zt)
    gs[...] = jnp.zeros_like(gs)

    for t in range(tiles):
        pad[t, 0:8, :] = rim_ref[:, t * 128 : t * 128 + 128].astype(f32)
        pad[t, 8 : 8 + c, :] = act_ref[t, 0:c, :].astype(f32)
    for t in range(tiles):

        def put(where, y):
            fresh0[t, where, :] = y

        conv_tile(pad, taps, t, key_heads, put)
    for t in range(tiles):
        act0[t] = fresh0[t].astype(bf16)
    for b in range(tokens // c):
        rows = slice(b * c, (b + 1) * c)
        dl = dl_ref[:, rows]
        crow[b] = mm_exact(dl, upper)
        l_row = mm_exact(dl, ones)
        c_col = mm_exact(lower, dl, NT)
        b_col = mm_exact(eye, wb_ref[:, rows], NT)
        ec = jnp.exp(c_col)
        for n, x in enumerate((c_col, b_col, ec, b_col * ec, jnp.exp(c_col[c - 1 : c, :] - c_col))):
            cols[b, n] = x
        gams[b] = jnp.exp(gs[...])
        els[b] = jnp.exp(l_row)
        gs[...] = gs[...] + l_row

    def expand(part):
        return jnp.concatenate([part * m for m in band16], 0)

    def halves(s):
        return [(i, i + s) for i in range(s, c, 2 * s)]

    def mixing(b, act, rows):
        c_row = crow[b]
        c_col, b_col, ec, be, tail = (cols[b, n] for n in range(5))
        for kh in range(key_heads):
            qb = act[kh, rows, :]
            kb = act[key_heads + kh, rows, :]
            q = qb.astype(f32)
            k = kb.astype(f32)
            gram = mm(kb, kb, NT)
            qk = mm(qb, kb, NT)
            for r in range(ratio):
                h = kh * ratio + r
                at = b * heads + h
                diff = c_col[:, h : h + 1] - c_row[h : h + 1, :]
                spread = jnp.exp(jnp.where(xor >= 0, diff, -1e30))
                beta = b_col[:, h : h + 1]
                lm[at] = (beta * gram * spread).astype(bf16)
                qa[at, :, 0:DK] = (ec[:, h : h + 1] * q).astype(bf16)
                qa[at, :, DK : DK + c] = (qk * spread).astype(bf16)
                ke[at] = (be[:, h : h + 1] * k).astype(bf16)
                kt[at] = (tail[:, h : h + 1] * k).astype(bf16)
                bv[at] = (beta * act[2 * key_heads + h, rows, :].astype(f32)).astype(bf16)

    def later(b, unused):
        mixing(b, act_ref, pl.ds(pl.multiple_of(b * c, c), c))
        return unused

    mixing(0, act0, slice(0, c))
    lax.fori_loop(1, tokens // c, later, 0)

    def flag(m):
        return m.astype(f32).astype(bf16)

    base16 = flag(cx == 0)
    pick16 = {s: flag((cx >= s) & (cx < 2 * s)) for s in (1, 2, 4, 8)}
    pick_rows = {}
    for s in (16, 32, 64):
        part = jnp.concatenate([xor[i:j] for i, j in halves(s)], 0)
        pick_rows[s] = flag((part >= s) & (part < 2 * s))

    def paired(left, right):
        out = []
        for n in range(0, GROUP, 2):
            both = mm(
                jnp.concatenate([left[n], left[n + 1]], 0),
                jnp.concatenate([expand(right[n]), expand(right[n + 1])], 1),
            ).astype(bf16)
            out += [both[0:SUB, 0:c], both[SUB : 2 * SUB, c : 2 * c]]
        return out

    def invert(g, unused):
        group = [g * GROUP + n for n in range(GROUP)]
        small = []
        for h in group:
            lc = lm[h, 0:SUB, :] * band16[0]
            for b in range(1, c // SUB):
                lc = lc + lm[h, b * SUB : (b + 1) * SUB, :] * band16[b]
            small.append(lc)
        tc = [base16 - lc * pick16[1] for lc in small]
        s = 2
        while s < SUB:
            rc = paired([lc * pick16[s] for lc in small], tc)
            fix = paired(tc, rc)
            tc = [tc[n] - fix[n] for n in range(GROUP)]
            s *= 2
        for n, h in enumerate(group):
            tm[h] = expand(tc[n])
        while s < c:
            half = halves(s)
            zero = jnp.zeros((s, c), bf16)
            rr = []
            for h in group:
                sub = jnp.concatenate([lm[h, i:j, :] for i, j in half], 0)
                rr.append(mm(sub * pick_rows[s], tm[h]).astype(bf16))
            for r, h in zip(rr, group):
                full = []
                for n in range(len(half)):
                    full += [zero, r[n * s : (n + 1) * s]]
                sub = jnp.concatenate([tm[h, i:j, :] for i, j in half], 0)
                sub = sub - mm(sub, jnp.concatenate(full, 0)).astype(bf16)
                for n, (i, j) in enumerate(half):
                    tm[h, i:j, :] = sub[n * s : (n + 1) * s]
            s *= 2
        return unused

    lax.fori_loop(0, tokens // c * heads // GROUP, invert, 0)

    def chunk(b, unused):
        rows = pl.ds(pl.multiple_of(b * c, c), c)
        gam = gams[b]
        el = els[b]
        for h in range(heads):
            at = b * heads + h
            kef = ke[at]
            y = mm(kef, zt[h].astype(bf16))
            yb[h, :, 0:DV] = (bv[at].astype(f32) - y[:, :DV]).astype(bf16)
            yb[h, :, DV:] = (gam[h : h + 1, :] * kef.astype(f32) - y[:, DV:]).astype(bf16)
        for h in range(heads):
            fb[h] = mm(tm[b * heads + h], yb[h]).astype(bf16)
        for h in range(heads):
            at = b * heads + h
            z = zt[h]
            fresh = fb[h]
            both = jnp.concatenate([z.astype(bf16), fresh], 0)
            out = mm(qa[at], both)
            o_ref[rows, h * DV : (h + 1) * DV] = out[:, :DV].astype(bf16)
            qe_ref[rows, h * DK : (h + 1) * DK] = (
                gam[h : h + 1, :] * qa[at, :, 0:DK].astype(f32) - out[:, DV:]
            ).astype(bf16)
            scale = el[h : h + 1, :]
            zt[h] = jnp.concatenate([scale, scale], 1) * z + mm(kt[at], fresh, TN)
        return unused

    lax.fori_loop(0, tokens // c, chunk, 0)
    for h in range(heads):
        z = zt[h]
        x_ref[h, 0:DK, :] = z[:, :DV].astype(bf16)
        x_ref[h, DK : 2 * DK, :] = z[:, DV:].astype(bf16)
        x_ref[h, 2 * DK : 2 * DK + EXTRA, :] = extras(gs[h : h + 1, :])


def prep(act, taps, rim, dl, wb):
    tiles, tokens, _ = act.shape
    h = dl.shape[0]
    vw = h * DV
    c = CHUNK
    n = tokens // c
    return pl.pallas_call(
        prep_kernel,
        in_specs=[VMEM_SPEC] * 5,
        out_shape=(
            pltpu.VMEM((tokens, vw), bf16),
            pltpu.VMEM((tokens, h * DK), bf16),
            pltpu.HBM((h, 2 * DK + EXTRA, DV), bf16),
        ),
        scratch_shapes=[
            pltpu.VMEM((tiles, c + 8, 128), f32),
            pltpu.VMEM((tiles, c, 128), f32),
            pltpu.VMEM((tiles, c, 128), bf16),
            pltpu.VMEM((n, 5, c, h), f32),
            pltpu.VMEM((n, h, 128), f32),
            pltpu.VMEM((n * h, c, c), bf16),
            pltpu.VMEM((n * h, c, c), bf16),
            pltpu.VMEM((n * h, c, DK + c), bf16),
            pltpu.VMEM((n * h, c, DK), bf16),
            pltpu.VMEM((n * h, c, DK), bf16),
            pltpu.VMEM((n * h, c, DV), bf16),
            pltpu.VMEM((n, h, 128), f32),
            pltpu.VMEM((n, h, 128), f32),
            pltpu.VMEM((h, c, DV + DK), bf16),
            pltpu.VMEM((h, c, DV + DK), bf16),
            pltpu.VMEM((h, DK, DV + DK), f32),
            pltpu.VMEM((8, 128), f32),
        ],
        compiler_params=params(24),
        name="prep",
    )(*(local(x) for x in (act, taps, rim, dl, wb)))


def log_decay(ref, at):
    rows = ref[at, 2 * DK : 2 * DK + EXTRA, :].astype(f32)
    return rows[0:1, :] + rows[1:2, :] + rows[2:3, :]


def row_kernel(x_ref, pre_ref, g_ref, out_ref):
    count = x_ref.shape[0]
    z = jnp.zeros((DK, DV + DK), f32)
    g = jnp.zeros((1, DV), f32)
    for i in range(count):
        pre_ref[i] = z.astype(bf16)
        g_ref[i] = jnp.broadcast_to(g, (8, DV))
        step = log_decay(x_ref, i)
        d = x_ref[i, DK : 2 * DK, :]
        scale = jnp.broadcast_to(jnp.exp(step), (DK, DV))
        past = jnp.broadcast_to(jnp.exp(g), (DK, DV))
        add = jnp.concatenate([x_ref[i, 0:DK, :].astype(f32), past * d.astype(f32)], 1)
        z = jnp.concatenate([scale, scale], 1) * z - mm(d, z.astype(bf16)) + add
        g = g + step
    out_ref[0:DK, :] = z[:, :DV].astype(bf16)
    out_ref[DK : 2 * DK, :] = z[:, DV:].astype(bf16)
    out_ref[2 * DK : 2 * DK + EXTRA, :] = extras(g)


def row_prefix(x):
    count = x.shape[0]
    return pl.pallas_call(
        row_kernel,
        out_shape=(
            pltpu.VMEM((count, DK, DV + DK), bf16),
            pltpu.VMEM((count, 8, DV), f32),
            pltpu.VMEM((2 * DK + EXTRA, DV), bf16),
        ),
        compiler_params=params(8),
        name="row_prefix",
    )(x)


def start_kernel(y_ref, a_ref, b_ref, c_ref, pre_ref, g_ref, out_ref):
    count = pre_ref.shape[0]
    s = jnp.zeros((DK, DV), f32)
    y = y_ref[0]
    for back, ref in ((3, a_ref), (2, b_ref), (1, c_ref)):
        rows = ref[2 * DK : 2 * DK + EXTRA, :].astype(f32)
        step = rows[0:1, :] + rows[1:2, :] + rows[2:3, :]
        scale = jnp.broadcast_to(jnp.exp(step), (DK, DV))
        after = scale * s - mm(ref[DK : 2 * DK, :], s.astype(bf16)) + ref[0:DK, :].astype(f32)
        s = jnp.where(y >= back, after, s)
    sb = s.astype(bf16)
    for i in range(count):
        z = pre_ref[i]
        scale = jnp.broadcast_to(jnp.exp(g_ref[i, 0:1, :]), (DK, DV))
        out_ref[i] = (scale * s - mm(z[:, DV:], sb) + z[:, :DV].astype(f32)).astype(bf16)


def start_states(y, a, b, c, pre, g):
    count = pre.shape[0]
    return pl.pallas_call(
        start_kernel,
        in_specs=[SMEM_SPEC] + [VMEM_SPEC] * 5,
        out_shape=pltpu.HBM((count, DK, DV), bf16),
        compiler_params=params(8),
        name="start_states",
    )(y, *(local(x) for x in (a, b, c, pre, g)))


def block(w_ref, z_ref, d):
    width = w_ref.shape[1] // 4
    at = pl.multiple_of(((z_ref[0] + d) & 3) * width, width)
    return w_ref[:, pl.ds(at, width)]


def hide(o_ref, qe_ref, s_ref, gate_ref, gain_ref, hid_ref, half):
    rows = slice(half * hid_ref.shape[0], (half + 1) * hid_ref.shape[0])
    gain = gain_ref[...]
    for h in range(s_ref.shape[0]):
        cols = slice(h * DV, (h + 1) * DV)
        x = o_ref[rows, cols].astype(f32) + mm(qe_ref[rows, cols], s_ref[h])
        x = x * lax.rsqrt(jnp.mean(x * x, -1, keepdims=True) + 1e-06)
        hid_ref[:, cols] = (x * gain * silu(gate_ref[:, cols].astype(f32))).astype(bf16)


def first_kernel(
    z_ref, o_ref, qe_ref, s_ref, gain_ref, gate_ref, w_ref, hid_ref, far_ref, wb_ref, gate_b, gate_a, sem
):
    width = wb_ref.shape[1]
    half = hid_ref.shape[0]
    at = pl.multiple_of(((z_ref[0] + 2) & 3) * width, width)
    fetch_a = pltpu.make_async_copy(gate_ref.at[0:half, :], gate_a, sem.at[0])
    fetch_w = pltpu.make_async_copy(w_ref.at[:, pl.ds(at, width)], wb_ref, sem.at[1])
    fetch_b = pltpu.make_async_copy(gate_ref.at[half : 2 * half, :], gate_b, sem.at[2])
    fetch_a.start()
    fetch_w.start()
    fetch_b.start()
    fetch_a.wait()
    hide(o_ref, qe_ref, s_ref, gate_a, gain_ref, hid_ref, 0)
    fetch_w.wait()
    far_ref[...] = mm(hid_ref[...], wb_ref[...]).astype(bf16)
    fetch_b.wait()


def second_kernel(o_ref, qe_ref, s_ref, gate_ref, gain_ref, wb_ref, hid_ref, far_ref):
    hide(o_ref, qe_ref, s_ref, gate_ref, gain_ref, hid_ref, 1)
    far_ref[...] = mm(hid_ref[...], wb_ref[...]).astype(bf16)


def first_half(z, o, qe, s, gate, gain, w):
    tokens, vw = o.shape
    width = w.shape[1] // 4
    return pl.pallas_call(
        first_kernel,
        in_specs=[SMEM_SPEC] + [VMEM_SPEC] * 4 + [pl.BlockSpec(memory_space=pl.ANY)] * 2,
        out_shape=[
            pltpu.VMEM((tokens // 2, vw), bf16),
            pltpu.VMEM((tokens // 2, width), bf16),
            pltpu.VMEM((vw, width), bf16),
            pltpu.VMEM((tokens // 2, vw), bf16),
        ],
        scratch_shapes=[pltpu.VMEM((tokens // 2, vw), bf16), pltpu.SemaphoreType.DMA((3,))],
        compiler_params=params(8),
        name="first_half",
    )(z, *(local(x) for x in (o, qe, s, gain)), far(gate), far(w))


def second_half(o, qe, s, gate, gain, wb):
    tokens, vw = o.shape
    return pl.pallas_call(
        second_kernel,
        in_specs=[VMEM_SPEC] * 6,
        out_shape=[
            pltpu.VMEM((tokens // 2, vw), bf16),
            pltpu.VMEM((tokens // 2, wb.shape[1]), bf16),
        ],
        compiler_params=params(8),
        name="second_half",
    )(*(local(x) for x in (o, qe, s, gate, gain, wb)))


def block(w_ref, z_ref, d):
    width = w_ref.shape[1] // 4
    at = pl.multiple_of(((z_ref[0] + d) & 3) * width, width)
    return w_ref[:, pl.ds(at, width)]


def parts_kernel(z_ref, a_ref, b_ref, w_ref, *outs, jobs):
    for (half, d), out in zip(jobs, outs):
        out[...] = mm((b_ref if half else a_ref)[...], block(w_ref, z_ref, d)).astype(out.dtype)


def parts(z, hid_a, hid_b, w, jobs, kinds):
    tokens = hid_a.shape[0]
    width = w.shape[1] // 4
    return pl.pallas_call(
        functools.partial(parts_kernel, jobs=jobs),
        in_specs=[SMEM_SPEC] + [VMEM_SPEC] * 3,
        out_shape=[pltpu.VMEM((tokens, width), kind) for kind in kinds],
        compiler_params=params(16),
        name="parts",
    )(z, local(hid_a), local(hid_b), local(w))


def finish_kernel(own_a, near_a, sum_a, own_b, near_b, sum_b, out_ref):
    half = own_a.shape[0]
    for at, group in ((0, (own_a, near_a, sum_a)), (half, (own_b, near_b, sum_b))):
        total = sum(ref[...].astype(f32) for ref in group)
        out_ref[at : at + half, :] = total.astype(bf16)


def finish(*pieces):
    rows, width = pieces[0].shape
    return pl.pallas_call(
        finish_kernel,
        in_specs=[VMEM_SPEC] * 6,
        out_shape=jax.ShapeDtypeStruct((2 * rows, width), bf16),
        compiler_params=params(8),
        name="finish",
    )(*(local(x) for x in pieces))


def body(q, k, v, cq, ck, cv, decay_log, write_beta, gate, gain, out_weight):
    tokens = q.shape[0]
    ctx = lax.axis_size("ctx")
    rows = ctx // ROW
    idx = lax.axis_index("ctx")
    z = lax.axis_index("head")
    rim = lax.ppermute(tails(q, k, v), "ctx", [(i, i + 1) for i in range(ctx - 1)])
    act, taps = acts(q, k, v, cq, ck, cv)
    o, qe, x = prep(act, taps, rim, decay_log, write_beta)
    groups = [[y * ROW + j for j in range(ROW)] for y in range(rows)]
    mine = lax.all_to_all(x, "ctx", 0, 0, axis_index_groups=groups, tiled=True)
    pre, g, whole = row_prefix(mine)

    def from_back(d):
        return lax.ppermute(whole, "ctx", [(i, (i + d * ROW) % ctx) for i in range(ctx)])

    s_mine = start_states((idx // ROW).reshape(1), from_back(3), from_back(2), from_back(1), pre, g)
    s = lax.all_to_all(s_mine, "ctx", 0, 0, axis_index_groups=groups, tiled=True)
    z = z.reshape(1)
    gain = gain.reshape(1, DV)
    ahead = lambda x: lax.ppermute(x, "head", [(i, (i + 1) % 4) for i in range(4)])
    behind = lambda x: lax.ppermute(x, "head", [(i, (i + 3) % 4) for i in range(4)])
    hid_a, far_a, wb, gate_b = first_half(z, o, qe, s, gate, gain, out_weight)
    far_a = ahead(far_a)
    hid_b, far_b = second_half(o, qe, s, gate_b, gain, wb)
    far_b = behind(far_b)
    jobs = ((1, 1), (0, 3), (0, 1), (1, 3))
    near_b, near_a, next_a, next_b = parts(z, hid_a, hid_b, out_weight, jobs, (bf16, bf16, f32, f32))
    near_b, near_a = ahead(near_b), behind(near_a)
    own_a, own_b = parts(z, hid_a, hid_b, out_weight, ((0, 0), (1, 0)), (f32, f32))
    sum_a = ahead((next_a + far_a.astype(f32)).astype(bf16))
    sum_b = behind((next_b + far_b.astype(f32)).astype(bf16))
    return finish(own_a, near_a, sum_a, own_b, near_b, sum_b)


def solution(mesh):
    return jax.shard_map(
        body,
        mesh=mesh,
        in_specs=(
            P("ctx", "head"), P("ctx", "head"), P("ctx", "head"),
            P(None, "head"), P(None, "head"), P(None, "head"),
            P("head", "ctx"), P("head", "ctx"), P("ctx", "head"), P(), P("head", None),
        ),
        out_specs=P("ctx", "head"),
        check_vma=False,
    )
```
